128 devices in a mesh: row: 8 (over z, core), col: 16 (over x, y).
Axes of the slice: x: 4, y: 4, z: 4, core: 2. Of those that a mesh axis runs over, the one named last changes fastest.
Arguments:
- layer_input: bfloat16 [1024, 8192], P('col', 'row'), may hold values from -6 to 6
- out_grad: bfloat16 [1024, 8192], P('col', 'row'), may hold values from -6 to 6
- gate_saved: bfloat16 [1024, 14336], P('row', 'col'), may hold values from -8 to 8
- up_saved: bfloat16 [1024, 14336], P('row', 'col'), may hold values from -6 to 6
- gate_weight: bfloat16 [8192, 14336], P('row', 'col'), may hold values from -0.0625 to 0.0625
- up_weight: bfloat16 [8192, 14336], P('row', 'col'), may hold values from -0.0625 to 0.0625
- down_weight: bfloat16 [14336, 8192], P('col', 'row'), may hold values from -0.046875 to 0.046875
Outputs:
- input_grad: bfloat16 [1024, 8192], P('col', 'row')
- gate_weight_grad: float32 [8192, 14336], P('row', 'col')
- up_weight_grad: float32 [8192, 14336], P('row', 'col')
- down_weight_grad: float32 [14336, 8192], P('col', 'row')
The draws below stay inside these ranges and needn't reach their ends.
All inputs are finite; a program needn't handle non-finite values.
Results may differ from the reference program's by a relative error of at most 0.02.
Values may be sent and summed in bfloat16 or wider, within the bound.
A program may use at most 128 MiB of HBM per device.

```python
import jax
import jax.numpy as jnp
from jax import lax

D = 8192
FF = 14336
TOKENS = 1024
N_COL = 16


def shard_levels(own_key, dims, shards, smallest, top_value):
    loudness, own = 1.0, jax.random.fold_in(own_key, 6)
    for axis_at, blocks in shards:
        draws = jnp.exp(jax.random.uniform(jax.random.fold_in(own, axis_at), (blocks,), jnp.float32, smallest / len(shards), top_value / len(shards)))
        loudness = loudness * jnp.repeat(draws, dims[axis_at] // blocks).reshape([-1 if axis == axis_at else 1 for axis in range(len(dims))])
    return loudness


def centred(rng, shape, spread, limit, cuts=(), kind=jnp.bfloat16):
    level = shard_levels(rng, shape, cuts, -0.22, 0.18) if cuts else 1.0
    values = jax.random.normal(rng, shape, jnp.float32) * spread * level
    return jnp.minimum(jnp.maximum(values, -limit), limit).astype(kind)


def setup_inputs(seed: int = 0) -> dict:
    key_of = jax.random.split(jax.random.key(seed), 8)
    layer_input = centred(key_of[0], (TOKENS, D), 1.0, 6.0, ((0, 16), (1, 8)))
    out_grad = centred(key_of[1], (TOKENS, D), 1.0, 6.0, ((0, 16), (1, 8)))
    gate_saved = centred(key_of[2], (TOKENS, FF), 1.5, 8.0, ((0, 8), (1, 16)))
    up_saved = centred(key_of[3], (TOKENS, FF), 1.0, 6.0, ((0, 8), (1, 16)))
    gate_weight = centred(key_of[4], (D, FF), D ** -0.5, 0.0625, ((0, 8), (1, 16)))
    up_weight = centred(key_of[5], (D, FF), D ** -0.5, 0.0625, ((0, 8), (1, 16)))
    down_weight = centred(key_of[6], (FF, D), FF ** -0.5, 0.046875, ((0, 16), (1, 8)))
    return dict(layer_input=layer_input, out_grad=out_grad, gate_saved=gate_saved, up_saved=up_saved, gate_weight=gate_weight, up_weight=up_weight, down_weight=down_weight)


def contract_last(left, right):
    return lax.dot_general(left, right, (((1,), (1,)), ((), ())), preferred_element_type=jnp.float32)


def contract_first(left, right):
    return lax.dot_general(left, right, (((0,), (0,)), ((), ())), preferred_element_type=jnp.float32)


def reference(layer_input, out_grad, gate_saved, up_saved, gate_weight, up_weight, down_weight):
    hidden_grad = contract_last(out_grad, down_weight)
    gate_val = gate_saved.astype(jnp.float32)
    up_val = up_saved.astype(jnp.float32)
    sigma = 1.0 / (1.0 + jnp.exp(-gate_val))
    silu_val = gate_val * sigma
    hidden = (silu_val * up_val).astype(jnp.bfloat16)
    gate_grad = (hidden_grad * up_val * sigma * (1.0 + gate_val * (1.0 - sigma))).astype(jnp.bfloat16)
    up_grad = (hidden_grad * silu_val).astype(jnp.bfloat16)
    ff_block = FF // N_COL
    input_total = jnp.zeros((TOKENS, D), jnp.float32)
    for block in range(N_COL):
        lower = block * ff_block
        upper = lower + ff_block
        block_term = contract_last(gate_grad[:, lower:upper], gate_weight[:, lower:upper]) + contract_last(up_grad[:, lower:upper], up_weight[:, lower:upper])
        input_total = input_total + block_term.astype(jnp.bfloat16).astype(jnp.float32)
    input_grad = input_total.astype(jnp.bfloat16)
    scale = float(TOKENS) ** -0.5
    gate_weight_grad = scale * contract_first(layer_input, gate_grad)
    up_weight_grad = scale * contract_first(layer_input, up_grad)
    down_weight_grad = scale * contract_first(hidden, out_grad)
    return input_grad, gate_weight_grad, up_weight_grad, down_weight_grad
```

```python
import jax
import jax.numpy as jnp
from jax import lax
from jax.experimental import pallas as pl
from jax.experimental.pallas import tpu as pltpu
from jax.sharding import PartitionSpec as P

BF = jnp.bfloat16
F32 = jnp.float32
MESH = pl.DeviceIdType.MESH
N_COPIES = 160
SIDES = (1, -1)


def kernel(
    x_hbm, dy_hbm, g_hbm, u_hbm, wg_hbm, wu_hbm, wd_hbm,
    ig_out, gw_out, uw_out, dw_out,
    x_all, dy_all, g_all, u_all, wg, wu, wd,
    slope, silu, hidden,
    part, part_in, chip_sum, half_in, full_in,
    hg_all, gg, ug,
    q, r2, rf, s1, t1, t2, r2b, rfb,
    send_sem, recv_sem, load_sem,
):
    r = lax.axis_index("row")
    c = lax.axis_index("col")
    z, core = lax.div(r, 2), lax.rem(r, 2)
    x, y = lax.div(c, 4), lax.rem(c, 4)
    up4 = lambda a, d: lax.rem(a + (d + 4), 4)
    col = lambda dx, dy: up4(x, dx) * 4 + up4(y, dy)
    row = lambda dz: up4(z, dz) * 2 + core
    row_other = lambda dz: up4(z, dz) * 2 + (1 - core)
    partner = {"row": row_other(0), "col": c}
    z_dev = lambda s: {"row": row(s), "col": c}

    loads = {}
    for i, (name, src, dst) in enumerate((
        ("dy", dy_hbm, dy_all.at[c]), ("g", g_hbm, g_all.at[r]), ("u", u_hbm, u_all.at[r]),
        ("wd", wd_hbm, wd), ("x", x_hbm, x_all.at[c]), ("wg", wg_hbm, wg), ("wu", wu_hbm, wu),
    )):
        loads[name] = pltpu.make_async_copy(src, dst, load_sem.at[i])
        loads[name].start()

    barrier = pltpu.get_barrier_semaphore()
    peers = [partner, z_dev(1), z_dev(-1)]
    peers += [{"row": r, "col": col(s, 0)} for s in SIDES]
    peers += [{"row": r, "col": col(0, s)} for s in SIDES]
    for p in peers:
        pl.semaphore_signal(barrier, inc=1, device_id=p, device_id_type=MESH)
    pl.semaphore_wait(barrier, len(peers))

    sent = []

    def send(src, dst, dev):
        i = len(sent)
        copy = pltpu.make_async_remote_copy(
            src_ref=src, dst_ref=dst, send_sem=send_sem.at[i], recv_sem=recv_sem.at[i],
            device_id=dev, device_id_type=MESH,
        )
        copy.start()
        sent.append(copy)
        return copy

    rows = (pl.ds(0, 32), pl.ds(32, 32))
    side_cols = {1: pl.ds(0, 512), -1: pl.ds(512, 512)}

    def at(h, a, b):
        return col(a, b) if h == 0 else col(b, a)

    def nb(h, dim, s):
        return {"row": r, "col": at(h, s, 0) if dim == 0 else at(h, 0, s)}

    def gather_xy(src, buf):
        m1, m2, r1, r2_ = {}, {}, {}, {}
        for h in range(2):
            for s in SIDES:
                m1[h, s] = send(src.at[rows[h]], buf.at[c, rows[h]], nb(h, 0, s))
        for h in range(2):
            for s in SIDES:
                m2[h, 0, s] = send(src.at[rows[h]], buf.at[c, rows[h]], nb(h, 1, s))
        yield
        for s in SIDES:
            for h in range(2):
                m1[h, s].wait_recv()
                slot = buf.at[at(h, -s, 0), rows[h]]
                piece = buf.at[at(h, -s, 0), rows[h], side_cols[s]]
                r1[h, s] = send(piece, piece, nb(h, 0, s))
                for t in SIDES:
                    m2[h, -s, t] = send(slot, slot, nb(h, 1, t))
                yield
        def relay(h, j, s):
            m2[h, j, s].wait_recv()
            piece = buf.at[at(h, j, -s), rows[h], side_cols[s]]
            r2_[h, j, s] = send(piece, piece, nb(h, 1, s))
        for h in range(2):
            for s in SIDES:
                relay(h, 0, s)
            yield
        for h in range(2):
            r1[h, 1].wait_recv()
            r1[h, -1].wait_recv()
            slot = buf.at[at(h, 2, 0), rows[h]]
            for t in SIDES:
                m2[h, 2, t] = send(slot, slot, nb(h, 1, t))
            yield
        for j in (-1, 1, 2):
            for h in range(2):
                for s in SIDES:
                    relay(h, j, s)
                yield
        for h in range(2):
            for j in (0, -1, 1, 2):
                for s in SIDES:
                    r2_[h, j, s].wait_recv()

    z_half = {1: pl.ds(0, 64), -1: pl.ds(64, 64)}

    def gather_z(src, buf, done):
        mine = buf.at[r]
        p0 = send(src, mine, partner)
        m = {s: send(src, mine, z_dev(s)) for s in SIDES}
        yield
        p0.wait_recv()
        done(0)
        yield
        rl, fw = {}, {}
        for s in SIDES:
            m[s].wait_recv()
            piece = buf.at[row(-s), z_half[s]]
            rl[s] = send(piece, piece, z_dev(s))
            fw[s] = send(buf.at[row(-s)], buf.at[row(-s)], partner)
            yield
        for s in SIDES:
            fw[s].wait_recv()
            done(-s)
            yield
        rl[1].wait_recv()
        rl[-1].wait_recv()
        far = send(buf.at[row(2)], buf.at[row(2)], partner)
        yield
        far.wait_recv()
        done(2)

    def factors(dz):
        first = up4(z, dz) * 2

        @pl.loop(0, 8)
        def _(i):
            slot = first + lax.div(i, 4)
            at_rows = pl.ds(lax.rem(i, 4) * 32, 32)
            gate = g_all[slot, at_rows, :].astype(F32)
            upv = u_all[slot, at_rows, :].astype(F32)
            sigma = 1.0 / (1.0 + jnp.exp(-gate))
            si = gate * sigma
            hidden[slot, at_rows, :] = (si * upv).astype(BF)
            silu[slot, at_rows, :] = si
            slope[slot, at_rows, :] = upv * sigma * (1.0 + gate * (1.0 - sigma))

    nothing = lambda dz: None

    def drain(gen):
        for _ in gen:
            pass

    ag_dy = gather_xy(dy_hbm, dy_all)
    next(ag_dy)
    ag_g = gather_z(g_hbm, g_all, nothing)
    next(ag_g)
    ag_u = gather_z(u_hbm, u_all, nothing)
    next(ag_u)
    loads["g"].wait()
    loads["u"].wait()
    next(ag_g)
    next(ag_u)
    factors(0)
    for _ in range(4):
        next(ag_dy)
    live = [ag_g, ag_u]
    k = 0
    for _ in ag_dy:
        if k % 2 == 0:
            next(live[0], None)
            next(live[1], None)
        k += 1
    loads["dy"].wait()
    loads["wd"].wait()

    ag_x = gather_xy(x_hbm, x_all)
    next(ag_x)

    zs = (2, 1, -1, 0)
    ps = {}
    for i, dz in enumerate(zs):
        first = up4(z, dz) * 4
        left = dy_all[pl.ds(first, 4)].reshape(256, 1024)
        prod = lax.dot_general(left, wd[...], (((1,), (1,)), ((), ())), preferred_element_type=F32)
        part[i] = prod.astype(BF).reshape(2, 128, 896)
        ps[dz] = send(part.at[i, 1 - core], part_in.at[i], partner)
        if i:
            next(ag_x)

    def chip(i, at_rows):
        return part[i, core, at_rows, :].astype(F32) + part_in[i, at_rows, :].astype(F32)

    drain(ag_g)
    drain(ag_u)
    ps[2].wait_recv()

    @pl.loop(0, 4)
    def _(k):
        at_rows = pl.ds(k * 32, 32)
        chip_sum[0, at_rows, :] = chip(0, at_rows).astype(BF)

    hs = {s: send(chip_sum.at[0, z_half[s]], half_in.at[z_half[s]], z_dev(s)) for s in SIDES}
    factors(-1)
    next(ag_x)
    fs = {}
    for n, s in enumerate(SIDES):
        ps[s].wait_recv()
        hs[s].wait_recv()
        lo = z_half[s].start

        @pl.loop(0, 4)
        def _(k):
            at_rows = pl.ds(k * 32, 32)
            chip_sum[1 + n, at_rows, :] = chip(1 + n, at_rows).astype(BF)

        @pl.loop(0, 2)
        def _(k):
            at_rows = pl.ds(lo + k * 32, 32)
            both = chip(1 + n, at_rows) + half_in[at_rows, :].astype(F32)
            chip_sum[1 + n, at_rows, :] = both.astype(BF)

        fs[s] = send(chip_sum.at[1 + n], full_in.at[n], z_dev(s))
    next(ag_x, None)
    factors(1)
    next(ag_x, None)
    factors(2)
    next(ag_x, None)
    ps[0].wait_recv()
    fs[1].wait_recv()
    fs[-1].wait_recv()

    @pl.loop(0, 4)
    def _(k):
        at_rows = pl.ds(k * 32, 32)
        total = chip(3, at_rows) + full_in[0, at_rows, :].astype(F32) + full_in[1, at_rows, :].astype(F32)
        hg_all[r, at_rows, :] = total.astype(BF)

    a2, a1 = {}, {}

    def stage1_far(h, b, slot):
        for s in SIDES:
            a2[h, b, s] = send(
                q.at[slot, rows[h], side_cols[s]], r2.at[h, b, :, side_cols[s]], e_nb(h, 0, s)
            )

    def e_nb(h, dim, s):
        return nb(1 - h, dim, s)

    def e_at(h, a, b_abs):
        return b_abs * 4 + up4(y, a) if h == 0 else up4(x, a) * 4 + b_abs

    def input_grad_block(dz):
        tb = up4(z, dz)

        @pl.loop(0, 8)
        def _(i):
            slot = tb * 2 + lax.div(i, 4)
            at_rows = pl.ds(lax.rem(i, 4) * 32, 32)
            hg = hg_all[slot, at_rows, :].astype(F32)
            gg[slot, at_rows, :] = (hg * slope[slot, at_rows, :]).astype(BF)
            ug[slot, at_rows, :] = (hg * silu[slot, at_rows, :]).astype(BF)

        nt = (((1,), (1,)), ((), ()))
        left_g = gg[pl.ds(tb * 2, 2)].reshape(256, 896)
        left_u = ug[pl.ds(tb * 2, 2)].reshape(256, 896)
        prod = lax.dot_general(left_g, wg[...], nt, preferred_element_type=F32)
        prod = prod + lax.dot_general(left_u, wu[...], nt, preferred_element_type=F32)
        q[pl.ds(tb * 4, 4)] = prod.astype(BF).reshape(4, 64, 1024)
        i = (0, -1, 1, 2).index(dz)
        for s in SIDES:
            a2[0, i, s] = send(
                q.at[e_at(0, 2, tb), rows[0], side_cols[s]],
                r2.at[0, i, :, side_cols[s]],
                e_nb(0, 0, s),
            )

    scale = float(x_all.shape[0] * x_all.shape[1]) ** -0.5
    tn = (((0,), (0,)), ((), ()))

    def down_grad(lo, n):
        left = hidden[:, :, lo : lo + n].reshape(1024, n)
        dw_out[lo : lo + n, :] = scale * lax.dot_general(
            left, dy_all[...].reshape(1024, 1024), tn, preferred_element_type=F32
        )

    def weight_grad(which, k):
        left = x_all[:, :, k * 256 : (k + 1) * 256].reshape(1024, 256)
        src, dst = (gg, gw_out) if which == 0 else (ug, uw_out)
        dst[k * 256 : (k + 1) * 256, :] = scale * lax.dot_general(
            left, src[...].reshape(1024, 896), tn, preferred_element_type=F32
        )

    loads["wg"].wait()
    loads["wu"].wait()
    ag_h = gather_z(hg_all.at[r], hg_all, input_grad_block)
    next(ag_h)
    down_grad(0, 384)
    next(ag_x, None)
    next(ag_h)
    next(ag_h)
    next(ag_h)
    next(ag_x, None)
    next(ag_x, None)
    down_grad(384, 512)
    next(ag_x, None)
    next(ag_x, None)
    next(ag_h)
    next(ag_h)
    next(ag_h)
    next(ag_x, None)
    next(ag_x, None)
    drain(ag_h)

    def q_rows(h, a, b_abs, cols=slice(None)):
        return q[e_at(h, a, b_abs), rows[h], cols].astype(F32)

    for j in range(4):
        for s in SIDES:
            a2[1, j, s] = send(
                q.at[e_at(1, 2, j), rows[1], side_cols[s]], r2.at[1, j, :, side_cols[s]], e_nb(1, 0, s)
            )
    drain(ag_x)
    loads["x"].wait()
    order_a = (0, -1, 1, 2)

    def b_abs(h, i):
        return up4(z, order_a[i]) if h == 0 else i

    a_sum = {}

    def near(h, i):
        for n, s in enumerate(SIDES):
            a2[h, i, s].wait_recv()
            sc, oc = side_cols[s], side_cols[-s]
            s1[h, i, n, :, sc] = (q_rows(h, s, b_abs(h, i), sc) + r2[h, i, :, sc].astype(F32)).astype(BF)
            s1[h, i, n, :, oc] = q[e_at(h, s, b_abs(h, i)), rows[h], oc]
            a1[h, i, s] = send(s1.at[h, i, n], rf.at[h, i, n], e_nb(h, 0, s))

    def mine(h, i):
        for s in SIDES:
            a1[h, i, s].wait_recv()
        b = b_abs(h, i)
        t1[h, b] = (
            q_rows(h, 0, b) + rf[h, i, 0].astype(F32) + rf[h, i, 1].astype(F32)
        ).astype(BF)

    for i in range(4):
        near(0, i)
    weight_grad(0, 0)
    for i in range(4):
        near(1, i)
    weight_grad(0, 1)
    weight_grad(0, 2)
    weight_grad(0, 3)
    c2, c1 = {}, {}
    own2 = (x, y)
    for h in range(2):
        for i in range(4):
            mine(h, i)
        for s in SIDES:
            far = up4(own2[h], 2)
            c2[h, s] = send(t1.at[h, far, :, side_cols[s]], r2b.at[h, :, side_cols[s]], e_nb(h, 1, s))
    weight_grad(1, 0)
    weight_grad(1, 1)
    for h in range(2):
        for n, s in enumerate(SIDES):
            c2[h, s].wait_recv()
            b = up4(own2[h], s)
            sc, oc = side_cols[s], side_cols[-s]
            t2[h, n, :, sc] = (t1[h, b, :, sc].astype(F32) + r2b[h, :, sc].astype(F32)).astype(BF)
            t2[h, n, :, oc] = t1[h, b, :, oc]
            c1[h, s] = send(t2.at[h, n], rfb.at[h, n], e_nb(h, 1, s))
    weight_grad(1, 2)
    weight_grad(1, 3)
    for h in range(2):
        for s in SIDES:
            c1[h, s].wait_recv()
        ig_out[rows[h], :] = (
            t1[h, own2[h]].astype(F32) + rfb[h, 0].astype(F32) + rfb[h, 1].astype(F32)
        ).astype(BF)
    for copy in sent:
        copy.wait_send()


def shards(layer_input, out_grad, gate_saved, up_saved, gate_weight, up_weight, down_weight):
    any_ = pl.BlockSpec(memory_space=pl.ANY)
    vm = pl.BlockSpec(memory_space=pltpu.VMEM)
    V = pltpu.VMEM
    return pl.pallas_call(
        kernel,
        out_shape=OUT_SHAPES,
        in_specs=[any_] * 7,
        out_specs=(vm,) * 4,
        scratch_shapes=[
            V((16, 64, 1024), BF), V((16, 64, 1024), BF),
            V((8, 128, 896), BF), V((8, 128, 896), BF),
            V((1024, 896), BF), V((1024, 896), BF), V((896, 1024), BF),
            V((8, 128, 896), F32), V((8, 128, 896), F32), V((8, 128, 896), BF),
            V((4, 2, 128, 896), BF), V((4, 128, 896), BF), V((3, 128, 896), BF),
            V((128, 896), BF), V((2, 128, 896), BF),
            V((8, 128, 896), BF), V((8, 128, 896), BF), V((8, 128, 896), BF),
            V((16, 64, 1024), BF),
            V((2, 4, 32, 1024), BF), V((2, 4, 2, 32, 1024), BF), V((2, 4, 2, 32, 1024), BF),
            V((2, 4, 32, 1024), BF), V((2, 2, 32, 1024), BF),
            V((2, 32, 1024), BF), V((2, 2, 32, 1024), BF),
            pltpu.SemaphoreType.DMA((N_COPIES,)),
            pltpu.SemaphoreType.DMA((N_COPIES,)),
            pltpu.SemaphoreType.DMA((7,)),
        ],
        compiler_params=pltpu.CompilerParams(
            collective_id=0, has_side_effects=True, vmem_limit_bytes=VLIM
        ),
        name="swiglu_backward",
    )(layer_input, out_grad, gate_saved, up_saved, gate_weight, up_weight, down_weight)


VLIM = 66_000_000
OUT_SHAPES = (
    jax.ShapeDtypeStruct((64, 1024), BF),
    jax.ShapeDtypeStruct((1024, 896), F32),
    jax.ShapeDtypeStruct((1024, 896), F32),
    jax.ShapeDtypeStruct((896, 1024), F32),
)


def solution(mesh):
    placed = (
        P("col", "row"), P("col", "row"), P("row", "col"), P("row", "col"),
        P("row", "col"), P("row", "col"), P("col", "row"),
    )
    return jax.shard_map(
        shards,
        mesh=mesh,
        in_specs=placed,
        out_specs=(P("col", "row"), P("row", "col"), P("row", "col"), P("col", "row")),
        check_vma=False,
    )
```
